32 devices in a mesh: lon: 8 (over y, x, core), lat: 4 (over z).
Axes of the slice: x: 2, y: 2, z: 4, core: 2. Of those that a mesh axis runs over, the one named last changes fastest.
Arguments:
- u_wind: float32 [256, 192, 1024], P(None, 'lat', 'lon'), may hold values from -40 to 40
- v_wind: float32 [256, 192, 1024], P(None, 'lat', 'lon'), may hold values from -40 to 40
Outputs:
- eof_basis: float32 [256, 2, 192, 1024], P(None, None, 'lat', 'lon')
- r_factor: float32 [256, 256], replicated
The draws below stay inside these ranges and needn't reach their ends.
All inputs are finite; a program needn't handle non-finite values.
Results may differ from the reference program's by a relative error of at most 0.00022.
Values sent between devices are 32-bit elements; how exact they have to be, the bound alone decides.
No kernel may reach another device: no remote copies, remote signals or barrier semaphores. Data moves between devices by JAX's collectives and lax.ppermute only.
A program may use at most 256 MiB of HBM per device.

```python
import jax
import jax.numpy as jnp
from jax import lax

SNAP = 256
NLAT = 192
NLON = 1024


def make_wind(key, which):
    base = jax.random.fold_in(key, which)
    common_key = jax.random.fold_in(key, 77)
    noise_key, amp_key, scale_key = jax.random.split(base, 3)
    noise = jnp.clip(jax.random.normal(noise_key, (SNAP, NLAT, NLON), jnp.float32), -4.0, 4.0)
    spread = jnp.log(3.0)
    common = jnp.clip(jax.random.normal(common_key, (NLAT, NLON), jnp.float32), -4.0, 4.0)
    amplitude = jax.random.uniform(amp_key, (SNAP, 1, 1), jnp.float32, 0.3, 1.0)
    lat_scale = jnp.exp(jax.random.uniform(scale_key, (1, NLAT, 1), jnp.float32, 0.0, 1.0) * spread)
    angle = jnp.arange(NLON).astype(jnp.float32) * (2.0 * jnp.pi / NLON)
    lon_scale = jnp.exp(0.55 * (1.0 + jnp.sin(angle)))[None, None, :]
    field = (noise + amplitude * common) * lat_scale * lon_scale
    return jnp.clip(field, -40.0, 40.0)


def draw_u_wind(key, part):
    return make_wind(key, 1)


def draw_v_wind(key, part):
    return make_wind(key, 2)


def setup_inputs(seed: int = 0) -> dict:
    arg_keys = jax.random.split(jax.random.key(seed), 3)
    return {
        "u_wind": draw_u_wind(jax.random.fold_in(arg_keys[2], 71), 0),
        "v_wind": draw_v_wind(jax.random.fold_in(arg_keys[2], 71), 0),
    }


def centred(padded, axis, count):

    def part(lo):
        return lax.slice_in_dim(padded, lo, lo + count, axis=axis)
    return (8.0 * (part(3) - part(1)) - (part(4) - part(0))) / 12.0

def one_snapshot(pair):
    u_one, v_one = pair
    rows = jnp.arange(-2, NLAT + 2).astype(jnp.float32)
    phi = -jnp.pi / 2 + (rows + 0.5) * jnp.pi / NLAT
    cosine = jnp.cos(phi)[:, None]
    middle = cosine[2:-2]
    ratio = NLON / (2.0 * NLAT)
    u_lon = jnp.pad(u_one, ((0, 0), (2, 2)), mode='wrap')
    v_lon = jnp.pad(v_one, ((0, 0), (2, 2)), mode='wrap')
    u_lat = jnp.pad(u_one, ((2, 2), (0, 0))) * cosine
    v_lat = jnp.pad(v_one, ((2, 2), (0, 0))) * cosine
    root = jnp.sqrt(middle)
    zeta = (ratio * centred(v_lon, 1, NLON) - centred(u_lat, 0, NLAT)) / root
    delta = (ratio * centred(u_lon, 1, NLON) + centred(v_lat, 0, NLAT)) / root
    return jnp.stack([zeta, delta]).reshape(-1)

def reference(u_wind, v_wind):
    matrix = lax.map(one_snapshot, (u_wind, v_wind))
    total = 2.0 * NLAT * NLON
    gram = lax.dot_general(matrix.astype(jnp.float32), matrix.astype(jnp.float32), (((1,), (1,)), ((), ())), precision=lax.Precision.HIGHEST, preferred_element_type=jnp.float32) / total
    lower = jnp.linalg.cholesky(gram)
    inverse = jax.scipy.linalg.solve_triangular(lower, jnp.eye(SNAP, dtype=jnp.float32), lower=True)
    basis = jnp.dot(inverse.astype(jnp.float32), matrix.astype(jnp.float32), precision=lax.Precision.HIGHEST, preferred_element_type=jnp.float32)
    return (basis.reshape(SNAP, 2, NLAT, NLON), lower.T)
```

```python
import functools

import jax
import jax.numpy as jnp
from jax import lax
from jax.experimental import pallas as pl
from jax.experimental.pallas import tpu as pltpu
from jax.sharding import PartitionSpec as P

F32 = jnp.float32
BF16 = jnp.bfloat16
VMEM = pltpu.MemorySpace.VMEM
LANES = 128
HALF = 128
PIECE = HALF + 8
GROUP = 4


def vmem_spec():
    return pl.BlockSpec(memory_space=VMEM)


def smem_spec():
    return pl.BlockSpec(memory_space=pltpu.MemorySpace.SMEM)


def any_spec():
    return pl.BlockSpec(memory_space=pl.ANY)


def in_vmem(x):
    return pltpu.with_memory_space_constraint(x, VMEM)


def in_hbm(x):
    return pltpu.with_memory_space_constraint(x, pltpu.MemorySpace.HBM)


def cost(flops, nbytes):
    return pl.CostEstimate(flops=flops, bytes_accessed=nbytes, transcendentals=0)


def load_body(rows, u_ref, v_ref, ut_ref, vt_ref, west_ref, east_ref, sems):
    snaps = u_ref.shape[0]

    def copy(wind, j):
        src = (u_ref, v_ref)[wind]
        dst = (ut_ref, vt_ref)[wind]
        return pltpu.make_async_copy(src.at[:, j, :], dst.at[j], sems.at[wind, j])

    def start(j, carry):
        copy(0, j).start()
        copy(1, j).start()
        return carry

    lax.fori_loop(0, rows, start, 0)
    step = 64
    lane = lax.broadcasted_iota(jnp.int32, (step, LANES), 1)
    for wind in range(2):
        west_ref[wind] = jnp.zeros((snaps, LANES), F32)
        east_ref[wind] = jnp.zeros((snaps, LANES), F32)

    def pack(j, carry):
        mine = (lane // 2) == j
        for wind in range(2):
            copy(wind, j).wait()
            src = (ut_ref, vt_ref)[wind]
            for t in range(0, snaps, step):
                cells = src[j, t : t + step, :]
                west = pltpu.roll(cells, 2 * j, 1)
                east = pltpu.roll(cells, 2 * j + 2, 1)
                part = pl.ds(t, step)
                west_ref[wind, part, :] = jnp.where(mine, west, west_ref[wind, part, :])
                east_ref[wind, part, :] = jnp.where(mine, east, east_ref[wind, part, :])
        return carry

    lax.fori_loop(0, rows, pack, 0)


def load_and_pack(u, v):
    snaps, rows, cols = u.shape
    turned = VMEM((rows, snaps, cols), F32)
    packed = VMEM((2, snaps, LANES), F32)
    return pl.pallas_call(
        functools.partial(load_body, rows),
        out_shape=(turned, turned, packed, packed),
        in_specs=[any_spec(), any_spec()],
        out_specs=(vmem_spec(),) * 4,
        scratch_shapes=[pltpu.SemaphoreType.DMA((2, rows))],
        compiler_params=pltpu.CompilerParams(vmem_limit_bytes=8 << 20),
        cost_estimate=cost(u.size * 8, u.size * 8),
        name="load_and_pack",
    )(in_hbm(u), in_hbm(v))


def stencil_body(rows, ut_ref, vt_ref, north_ref, south_ref, coef_ref, x_ref):
    snaps = ut_ref.shape[1]
    step = 32

    def one_row(j, u_row, v_row, u_near, v_near):
        lon8, lon1 = coef_ref[j, 0], coef_ref[j, 1]
        lat = [coef_ref[j, 2 + k] for k in range(4)]
        for t in range(0, snaps, step):
            part = pl.ds(t, step)
            for out, (own, near, sign) in enumerate(
                ((v_row, u_near, -1.0), (u_row, v_near, 1.0))
            ):
                cells = own(part)
                one = pltpu.roll(cells, LANES - 1, 1) - pltpu.roll(cells, 1, 1)
                two = pltpu.roll(cells, LANES - 2, 1) - pltpu.roll(cells, 2, 1)
                along = lon8 * one - lon1 * two
                cross = (lat[1] * near[2](part) - lat[0] * near[1](part)) - (
                    lat[3] * near[3](part) - lat[2] * near[0](part)
                )
                x_ref[j, part, out * LANES : (out + 1) * LANES] = (
                    along + cross if sign > 0 else along - cross
                )

    def inner(ref, j):
        return lambda part: ref[j, part, :]

    def getter(ref, wind, j):
        if j < 0:
            return inner(north_ref, wind * 2 + j + 2)
        if j >= rows:
            return inner(south_ref, wind * 2 + j - rows)
        return inner(ref, j)

    def edge(j):
        u_near = [getter(ut_ref, 0, j + d) for d in (-2, -1, 1, 2)]
        v_near = [getter(vt_ref, 1, j + d) for d in (-2, -1, 1, 2)]
        one_row(j, inner(ut_ref, j), inner(vt_ref, j), u_near, v_near)

    def middle(j, carry):
        u_near = [inner(ut_ref, j + d) for d in (-2, -1, 1, 2)]
        v_near = [inner(vt_ref, j + d) for d in (-2, -1, 1, 2)]
        one_row(j, inner(ut_ref, j), inner(vt_ref, j), u_near, v_near)
        return carry

    lax.fori_loop(2, rows - 2, middle, 0)
    for j in (0, 1, rows - 2, rows - 1):
        edge(j)


def differences(ut, vt, north, south, coef):
    rows, snaps, cols = ut.shape
    return pl.pallas_call(
        functools.partial(stencil_body, rows),
        out_shape=VMEM((rows, snaps, 2 * cols), F32),
        in_specs=[vmem_spec()] * 4 + [smem_spec()],
        out_specs=vmem_spec(),
        compiler_params=pltpu.CompilerParams(vmem_limit_bytes=8 << 20),
        cost_estimate=cost(ut.size * 26, ut.size * 16),
        name="differences",
    )(in_vmem(ut), in_vmem(vt), in_vmem(north), in_vmem(south), coef)


def gram_body(
    rows, x_ref, west_ref, east_ref, from_west_ref, from_east_ref, scale_ref,
    hi_ref, lo_ref, out_ref, fix_ref, acc_ref,
):
    snaps = x_ref.shape[1]
    step = 64
    lane = lax.broadcasted_iota(jnp.int32, (step, LANES), 1)
    even = lane % 2 == 0
    even_row = (lane // 2) % 2 == 0
    scale = scale_ref[0:1, :]
    for wind in range(2):
        for t in range(0, snaps, step):
            part = pl.ds(t, step)
            left = from_west_ref[wind, part, :] - east_ref[wind, part, :]
            right = from_east_ref[wind, part, :] - west_ref[wind, part, :]
            left = scale * (left - jnp.where(even, 8.0 * pltpu.roll(left, LANES - 1, 1), 0.0))
            right = scale * (jnp.where(even, 0.0, 8.0 * pltpu.roll(right, 1, 1)) - right)
            right = pltpu.roll(right, LANES - 2, 1)
            fix_ref[wind, 0, part, :] = jnp.where(even_row, left, right)
            fix_ref[wind, 1, part, :] = jnp.where(even_row, right, left)
    acc_ref[...] = jnp.zeros_like(acc_ref)
    outer = jnp.logical_or(lane < 2, lane >= LANES - 2)

    def group(i, carry):
        base = i * GROUP
        for k in range(GROUP):
            j = base + k
            shift = lax.rem(2 * LANES - 2 * j, LANES)
            for out in range(2):
                for t in range(0, snaps, step):
                    part = pl.ds(t, step)
                    fix = pltpu.roll(fix_ref[1 - out, k % 2, part, :], shift, 1)
                    span = slice(out * LANES, (out + 1) * LANES)
                    x = x_ref[j, part, span] + jnp.where(outer, fix, 0.0)
                    hi = x.astype(BF16)
                    hi_ref[j, part, span] = hi
                    lo_ref[j, part, span] = (x - hi.astype(F32)).astype(BF16)
        total = None
        for k in range(GROUP):
            hi = hi_ref[base + k]
            both = jnp.concatenate([hi, lo_ref[base + k]], axis=0)
            term = lax.dot_general(
                hi, both, (((1,), (1,)), ((), ())), preferred_element_type=F32
            )
            total = term if total is None else total + term
        acc_ref[...] += total
        return carry

    lax.fori_loop(0, rows // GROUP, group, 0)
    low = acc_ref[:, snaps:]
    gram = acc_ref[:, :snaps] + (low + low.T)
    row = lax.broadcasted_iota(jnp.int32, (HALF, HALF), 0)
    col = lax.broadcasted_iota(jnp.int32, (HALF, HALF), 1)
    first = gram[:HALF, :HALF]
    second = gram[HALF:, HALF:]
    out_ref[0, :HALF, :] = gram[HALF:, :HALF]
    out_ref[1, :HALF, :] = jnp.where(row >= col, first, second)
    diagonal = jnp.sum(jnp.where(row == col, second, 0.0), axis=0, keepdims=True)
    out_ref[0, HALF:, :] = jnp.broadcast_to(diagonal, (8, HALF))
    out_ref[1, HALF:, :] = jnp.zeros((8, HALF), F32)


def partial_gram(x, west, east, from_west, from_east, scale):
    rows, snaps, both = x.shape
    halves = VMEM((rows, snaps, both), BF16)
    return pl.pallas_call(
        functools.partial(gram_body, rows),
        out_shape=(halves, halves, VMEM((2, PIECE, HALF), F32)),
        in_specs=[vmem_spec()] * 6,
        out_specs=(vmem_spec(),) * 3,
        scratch_shapes=[
            pltpu.VMEM((2, 2, snaps, LANES), F32),
            pltpu.VMEM((snaps, 2 * snaps), F32),
        ],
        compiler_params=pltpu.CompilerParams(vmem_limit_bytes=12 << 20),
        cost_estimate=cost(x.size * 1024, x.size * 8),
        name="partial_gram",
    )(in_vmem(x), in_vmem(west), in_vmem(east), in_vmem(from_west), in_vmem(from_east), scale)


def swap(x, axis, bit):
    count = lax.axis_size(axis)
    return lax.ppermute(x, axis, [(i, i ^ bit) for i in range(count)])


def powers(count):
    bit = 1
    while bit < count:
        yield bit
        bit *= 2


def summed(parts):
    odd = lax.axis_index("lon") % 2 == 1
    mine = jnp.where(odd, parts[1], parts[0])
    other = jnp.where(odd, parts[0], parts[1])
    mine = mine + swap(other, "lon", 1)
    for bit in powers(lax.axis_size("lat")):
        mine = mine + swap(mine, "lat", bit)
    for bit in powers(lax.axis_size("lon")):
        if bit > 1:
            mine = mine + swap(mine, "lon", bit)
    theirs = swap(mine, "lon", 1)
    return jnp.where(odd, theirs, mine), jnp.where(odd, mine, theirs)


def dot_nt(a, b):
    return lax.dot_general(
        a, b, (((1,), (1,)), ((), ())), precision=lax.Precision.HIGHEST, preferred_element_type=F32
    )


def dot_nn(a, b):
    return lax.dot_general(
        a, b, (((1,), (0,)), ((), ())), precision=lax.Precision.HIGHEST, preferred_element_type=F32
    )


def eliminate(matrix):
    size = matrix.shape[0]
    groups = size // 8
    row = lax.broadcasted_iota(jnp.int32, (8, size), 0)
    col = lax.broadcasted_iota(jnp.int32, (8, size), 1)
    work = [matrix[8 * g : 8 * g + 8, :] for g in range(groups)]
    right = [jnp.where(col == row + 8 * g, 1.0, 0.0) for g in range(groups)]
    for k in range(size):
        g, r = divmod(k, 8)
        pivot_row = jnp.broadcast_to(work[g][r : r + 1, :], (8, size))
        right_row = jnp.broadcast_to(right[g][r : r + 1, :], (8, size))
        pivot = jnp.broadcast_to(pivot_row[:, k : k + 1], (8, size))
        inverse = 1.0 / pivot
        for h in range(g, groups):
            factor = jnp.broadcast_to(work[h][:, k : k + 1], (8, size)) * inverse
            if h == g:
                factor = jnp.where(row > r, factor, 0.0)
            work[h] = work[h] - factor * pivot_row
            right[h] = right[h] - factor * right_row
    upper, lower = [], []
    for g in range(groups):
        diagonal = jnp.sum(jnp.where(col == row + 8 * g, work[g], 0.0), axis=1, keepdims=True)
        root = lax.rsqrt(diagonal)
        upper.append(jnp.where(col >= row + 8 * g, work[g] * root, 0.0))
        lower.append(right[g] * root)
    return jnp.concatenate(upper, axis=0), jnp.concatenate(lower, axis=0)


def factor_body(total, corner_ref, mixed_ref, r_ref, hi_ref, lo_ref):
    inv = 1.0 / total
    row = lax.broadcasted_iota(jnp.int32, (HALF, HALF), 0)
    col = lax.broadcasted_iota(jnp.int32, (HALF, HALF), 1)
    mixed = mixed_ref[:HALF, :] * inv
    corner = corner_ref[:HALF, :] * inv
    diagonal = corner_ref[HALF : HALF + 1, :] * inv
    turned = mixed.T
    first = jnp.where(row >= col, mixed, turned)
    second = jnp.where(row < col, mixed, jnp.where(row > col, turned, diagonal))
    r11, w11 = eliminate(first)
    l21 = dot_nt(corner, w11)
    r22, w22 = eliminate(second - dot_nt(l21, l21))
    w21 = -dot_nn(w22, dot_nn(l21, w11))
    zero = jnp.zeros((HALF, HALF), F32)
    r_ref[:HALF, :HALF] = r11
    r_ref[:HALF, HALF:] = l21.T
    r_ref[HALF:, :HALF] = zero
    r_ref[HALF:, HALF:] = r22
    for i, j, w in ((0, 0, w11), (0, 1, zero), (1, 0, w21), (1, 1, w22)):
        part = (slice(i * HALF, (i + 1) * HALF), slice(j * HALF, (j + 1) * HALF))
        hi = w.astype(BF16)
        hi_ref[part] = hi
        lo_ref[part] = (w - hi.astype(F32)).astype(BF16)


def factor(corner, mixed, total):
    snaps = 2 * HALF
    return pl.pallas_call(
        functools.partial(factor_body, total),
        out_shape=(
            VMEM((snaps, snaps), F32),
            VMEM((snaps, snaps), BF16),
            VMEM((snaps, snaps), BF16),
        ),
        in_specs=[vmem_spec()] * 2,
        out_specs=(vmem_spec(),) * 3,
        compiler_params=pltpu.CompilerParams(vmem_limit_bytes=12 << 20),
        cost_estimate=cost(1 << 26, 1 << 20),
        name="factor",
    )(in_vmem(corner), in_vmem(mixed))


def basis_body(rows, whi_ref, wlo_ref, hi_ref, lo_ref, out_ref, buf_ref, sems):
    slots = buf_ref.shape[0]
    cols = out_ref.shape[3]

    def copy(j, slot, part):
        return pltpu.make_async_copy(
            buf_ref.at[slot, :, pl.ds(part * cols, cols)],
            out_ref.at[:, part, j, :],
            sems.at[slot, part],
        )

    weights = jnp.concatenate([whi_ref[...], whi_ref[...], wlo_ref[...]], axis=1)

    def step(j, carry):
        slot = lax.rem(j, slots)

        @pl.when(j >= slots)
        def _():
            copy(j - slots, slot, 0).wait()
            copy(j - slots, slot, 1).wait()

        cells = jnp.concatenate([hi_ref[j], lo_ref[j], hi_ref[j]], axis=0)
        buf_ref[slot] = lax.dot_general(
            weights, cells, (((1,), (0,)), ((), ())), preferred_element_type=F32
        )
        copy(j, slot, 0).start()
        copy(j, slot, 1).start()
        return carry

    lax.fori_loop(0, rows, step, 0)

    def drain(j, carry):
        slot = lax.rem(j, slots)
        copy(j, slot, 0).wait()
        copy(j, slot, 1).wait()
        return carry

    lax.fori_loop(rows - slots, rows, drain, 0)


def basis(whi, wlo, hi, lo):
    rows, snaps, both = hi.shape
    cols = both // 2
    slots = 8
    return pl.pallas_call(
        functools.partial(basis_body, rows),
        out_shape=jax.ShapeDtypeStruct((snaps, 2, rows, cols), F32),
        in_specs=[vmem_spec()] * 4,
        out_specs=any_spec(),
        scratch_shapes=[
            pltpu.VMEM((slots, snaps, both), F32),
            pltpu.SemaphoreType.DMA((slots, 2)),
        ],
        compiler_params=pltpu.CompilerParams(vmem_limit_bytes=8 << 20),
        cost_estimate=cost(hi.size * 1536, hi.size * 8),
        name="basis",
    )(in_vmem(whi), in_vmem(wlo), in_vmem(hi), in_vmem(lo))


def rim(u, v, low, high):
    rows = jnp.stack([u[:, low:high, :], v[:, low:high, :]])
    return rows.transpose(0, 2, 1, 3).reshape(2 * (high - low), u.shape[0], u.shape[2])


def on_device(u, v):
    snaps, rows, cols = u.shape
    n_lat = rows * lax.axis_size("lat")
    lat, lon = lax.axis_size("lat"), lax.axis_size("lon")
    n_lon = cols * lon
    ratio = n_lon / (2.0 * n_lat)

    north = lax.ppermute(rim(u, v, rows - 2, rows), "lat", [(i, i + 1) for i in range(lat - 1)])
    south = lax.ppermute(rim(u, v, 0, 2), "lat", [(i + 1, i) for i in range(lat - 1)])

    index = (lax.axis_index("lat") * rows + jnp.arange(-2, rows + 2)).astype(F32)
    cosine = jnp.cos(-jnp.pi / 2 + (index + 0.5) * jnp.pi / n_lat)
    root = 1.0 / (12.0 * jnp.sqrt(cosine[2:-2]))
    along = ratio * root
    coef = jnp.stack(
        [
            8.0 * along,
            along,
            8.0 * cosine[1:-3] * root,
            8.0 * cosine[3:-1] * root,
            cosine[:-4] * root,
            cosine[4:] * root,
        ],
        axis=1,
    )
    scale = jnp.broadcast_to(
        jnp.pad(jnp.repeat(along, 2), (0, LANES - 2 * rows))[None, :], (8, LANES)
    )

    ut, vt, west, east = load_and_pack(u, v)
    from_west = lax.ppermute(east, "lon", [(i, (i + 1) % lon) for i in range(lon)])
    from_east = lax.ppermute(west, "lon", [((i + 1) % lon, i) for i in range(lon)])
    x = differences(ut, vt, north, south, coef)
    hi, lo, parts = partial_gram(x, west, east, from_west, from_east, scale)
    corner, mixed = summed(parts)
    r, whi, wlo = factor(corner, mixed, 2.0 * n_lat * n_lon)
    return basis(whi, wlo, hi, lo), r


def solution(mesh):
    in_specs = (P(None, "lat", "lon"), P(None, "lat", "lon"))
    out_specs = (P(None, None, "lat", "lon"), P())
    return jax.shard_map(
        on_device, mesh=mesh, in_specs=in_specs, out_specs=out_specs, check_vma=False
    )
```

```python
import functools

import jax
import jax.numpy as jnp
from jax import lax
from jax.experimental import pallas as pl
from jax.experimental.pallas import tpu as pltpu
from jax.sharding import PartitionSpec as P

F32 = jnp.float32
BF16 = jnp.bfloat16
VMEM = pltpu.MemorySpace.VMEM
LANES = 128
HALF = 128
PIECE = HALF + 8
GROUP = 4


def vmem_spec():
    return pl.BlockSpec(memory_space=VMEM)


def smem_spec():
    return pl.BlockSpec(memory_space=pltpu.MemorySpace.SMEM)


def any_spec():
    return pl.BlockSpec(memory_space=pl.ANY)


def in_vmem(x):
    return pltpu.with_memory_space_constraint(x, VMEM)


def in_hbm(x):
    return pltpu.with_memory_space_constraint(x, pltpu.MemorySpace.HBM)


def cost(flops, nbytes):
    return pl.CostEstimate(flops=flops, bytes_accessed=nbytes, transcendentals=0)


def rim_body(rows, u_ref, v_ref, low_ref, high_ref, sems):
    def copy(k):
        wind, side, d = k // 4, k // 2 % 2, k % 2
        row = d if side == 0 else rows - 2 + d
        return pltpu.make_async_copy(
            (u_ref, v_ref)[wind].at[:, row, :],
            (low_ref, high_ref)[side].at[2 * wind + d],
            sems.at[k],
        )

    for k in range(8):
        copy(k).start()
    for k in range(8):
        copy(k).wait()


def rims(u, v):
    snaps, rows, cols = u.shape
    rim = VMEM((4, snaps, cols), F32)
    return pl.pallas_call(
        functools.partial(rim_body, rows),
        out_shape=(rim, rim),
        in_specs=[any_spec(), any_spec()],
        out_specs=(vmem_spec(),) * 2,
        scratch_shapes=[pltpu.SemaphoreType.DMA((8,))],
        compiler_params=pltpu.CompilerParams(vmem_limit_bytes=1 << 20),
        cost_estimate=cost(0, 1 << 22),
        name="rims",
    )(in_hbm(u), in_hbm(v))


def row_copy(u_ref, v_ref, ut_ref, vt_ref, sems):
    def copy(wind, j):
        src = (u_ref, v_ref)[wind]
        dst = (ut_ref, vt_ref)[wind]
        return pltpu.make_async_copy(src.at[:, j, :], dst.at[j], sems.at[wind, j])

    def start(j, carry):
        copy(0, j).start()
        copy(1, j).start()
        return carry

    return copy, start


def edge_body(rows, u_ref, v_ref, west_ref, east_ref, ut_ref, vt_ref, sems):
    snaps = u_ref.shape[0]
    copy, start = row_copy(u_ref, v_ref, ut_ref, vt_ref, sems)
    lax.fori_loop(0, rows, start, 0)
    step = 32
    lane = lax.broadcasted_iota(jnp.int32, (step, LANES), 1)
    for wind in range(2):
        west_ref[wind] = jnp.zeros((snaps, LANES), F32)
        east_ref[wind] = jnp.zeros((snaps, LANES), F32)

    def pack(i, carry):
        base = i * GROUP
        for k in range(GROUP):
            copy(0, base + k).wait()
            copy(1, base + k).wait()
        for wind in range(2):
            src = (ut_ref, vt_ref)[wind]
            for t in range(0, snaps, step):
                part = pl.ds(t, step)
                west, east = west_ref[wind, part, :], east_ref[wind, part, :]
                for k in range(GROUP):
                    j = base + k
                    turned = pltpu.roll(src[j, part, :], 2 * j + 2, 1)
                    west = jnp.where((lane >> 1) == j + 1, turned, west)
                    east = jnp.where((lane >> 1) == j, turned, east)
                west_ref[wind, part, :] = west
                east_ref[wind, part, :] = east
        return carry

    lax.fori_loop(0, rows // GROUP, pack, 0)


def edges(u, v):
    snaps, rows, cols = u.shape
    packed = VMEM((2, snaps, LANES), F32)
    return pl.pallas_call(
        functools.partial(edge_body, rows),
        out_shape=(packed, packed),
        in_specs=[any_spec(), any_spec()],
        out_specs=(vmem_spec(),) * 2,
        scratch_shapes=[
            pltpu.VMEM((rows, snaps, cols), F32),
            pltpu.VMEM((rows, snaps, cols), F32),
            pltpu.SemaphoreType.DMA((2, rows)),
        ],
        compiler_params=pltpu.CompilerParams(vmem_limit_bytes=16 << 20),
        cost_estimate=cost(u.size * 8, u.size * 8),
        name="edges",
    )(in_hbm(u), in_hbm(v))


def band():
    size = 2 * LANES
    k = lax.broadcasted_iota(jnp.int32, (size, size), 0)
    n = lax.broadcasted_iota(jnp.int32, (size, size), 1)
    inside = jnp.logical_and((k >> 7) == (n >> 7), (k & (LANES - 1)) < LANES - 2)
    d = n - k
    taps = jnp.where(d == 1, 8.0, jnp.where(jnp.logical_or(d == 0, d == 2), -1.0, 0.0))
    return jnp.where(inside, taps, 0.0).astype(BF16)


def split(x):
    hi = x.astype(BF16)
    return hi, (x - hi.astype(F32)).astype(BF16)


def stencil_row(j, coef_ref, band_ref, u_near, v_near, store, snaps, step):
    lon = coef_ref[j, 0]
    lat = [coef_ref[j, 1 + k] for k in range(4)]

    def across(near, part):
        return (lat[1] * near[3](part) - lat[0] * near[1](part)) - (
            lat[3] * near[4](part) - lat[2] * near[0](part)
        )

    for t in range(0, snaps, step):
        part = pl.ds(t, step)
        ahead = []
        for near in (v_near, u_near):
            cells = near[2](part)
            ahead.append(pltpu.roll(cells, LANES - 2, 1) - cells)
        hi, lo = split(jnp.concatenate(ahead, axis=1))
        taps = band_ref[...]
        along = lax.dot_general(
            lo, taps, (((1,), (0,)), ((), ())), preferred_element_type=F32
        ) + lax.dot_general(hi, taps, (((1,), (0,)), ((), ())), preferred_element_type=F32)
        store(part, 0, lon * along[:, :LANES] - across(u_near, part))
        store(part, 1, lon * along[:, LANES:] + across(v_near, part))


def row_of(ref, j):
    return lambda part: ref[j, part, :]


STENCIL_STEP = 128
STENCIL_ROWS = 4


def stencil_body(rows, u_ref, v_ref, coef_ref, x_ref, ut_ref, vt_ref, band_ref, sems):
    snaps = u_ref.shape[0]
    copy, start = row_copy(u_ref, v_ref, ut_ref, vt_ref, sems)
    lax.fori_loop(0, rows, start, 0)
    band_ref[...] = band()

    def arrived(j):
        copy(0, j).wait()
        copy(1, j).wait()

    def middle(i, carry):
        base = 2 + i * STENCIL_ROWS
        for r in range(STENCIL_ROWS):
            arrived(base + r + 2)
        for r in range(STENCIL_ROWS):
            j = base + r

            def store(part, out, value, j=j):
                x_ref[j, part, out * LANES : (out + 1) * LANES] = value

            near = [
                [row_of(ref, j + d) for d in range(-2, 3)] for ref in (ut_ref, vt_ref)
            ]
            stencil_row(j, coef_ref, band_ref, *near, store, snaps, STENCIL_STEP)
        return carry

    for j in range(4):
        arrived(j)
    lax.fori_loop(0, (rows - 4) // STENCIL_ROWS, middle, 0)


def differences(u, v, coef):
    snaps, rows, cols = u.shape
    return pl.pallas_call(
        functools.partial(stencil_body, rows),
        out_shape=VMEM((rows, snaps, 2 * cols), F32),
        in_specs=[any_spec()] * 2 + [smem_spec()],
        out_specs=vmem_spec(),
        scratch_shapes=[
            pltpu.VMEM((rows, snaps, cols), F32),
            pltpu.VMEM((rows, snaps, cols), F32),
            pltpu.VMEM((2 * LANES, 2 * LANES), BF16),
            pltpu.SemaphoreType.DMA((2, rows)),
        ],
        compiler_params=pltpu.CompilerParams(vmem_limit_bytes=18 << 20),
        cost_estimate=cost(u.size * 2048, u.size * 16),
        name="differences",
    )(in_hbm(u), in_hbm(v), coef)


def gram_body(
    rows, x_ref, west_ref, east_ref, from_west_ref, from_east_ref, north_ref, south_ref,
    u_ref, v_ref, scale_ref, coef_ref,
    hi_ref, lo_ref, out_ref,
    fix_ref, acc_ref, rim_ref, xe_ref, band_ref, sems,
):
    snaps = x_ref.shape[1]
    step = 64

    def rim_copy(wind, k):
        row = k if k < 4 else rows - 8 + k
        return pltpu.make_async_copy(
            (u_ref, v_ref)[wind].at[:, row, :], rim_ref.at[wind, k], sems.at[wind, k]
        )

    for k in range(8):
        rim_copy(0, k).start()
        rim_copy(1, k).start()
    lane = lax.broadcasted_iota(jnp.int32, (step, LANES), 1)
    even = lane % 2 == 0
    even_row = (lane // 2) % 2 == 0
    scale = scale_ref[0:1, :]
    for wind in range(2):
        for t in range(0, snaps, step):
            part = pl.ds(t, step)
            left = pltpu.roll(west_ref[wind, part, :], LANES - 2, 1) - from_west_ref[wind, part, :]
            right = pltpu.roll(from_east_ref[wind, part, :], LANES - 2, 1) - east_ref[wind, part, :]
            left = scale * (jnp.where(even, 8.0 * pltpu.roll(left, LANES - 1, 1), 0.0) - left)
            right = scale * (jnp.where(even, 0.0, 8.0 * pltpu.roll(right, 1, 1)) - right)
            right = pltpu.roll(right, LANES - 2, 1)
            fix_ref[wind, 0, part, :] = jnp.where(even_row, left, right)
            fix_ref[wind, 1, part, :] = jnp.where(even_row, right, left)
    acc_ref[...] = jnp.zeros_like(acc_ref)
    outer = jnp.logical_or(lane < 2, lane >= LANES - 2)

    def group(row_list, parities, loads):
        for j, parity, load in zip(row_list, parities, loads):
            shift = (2 * LANES - 2 * j) % LANES
            for out in range(2):
                for t in range(0, snaps, step):
                    part = pl.ds(t, step)
                    fix = pltpu.roll(fix_ref[1 - out, parity, part, :], shift, 1)
                    span = slice(out * LANES, (out + 1) * LANES)
                    x = load(part, span) + jnp.where(outer, fix, 0.0)
                    hi, lo = split(x)
                    hi_ref[j, part, span] = hi
                    lo_ref[j, part, span] = lo
        total = None
        for j in row_list:
            hi = hi_ref[j]
            both = jnp.concatenate([hi, lo_ref[j]], axis=0)
            term = lax.dot_general(
                hi, both, (((1,), (1,)), ((), ())), preferred_element_type=F32
            )
            total = term if total is None else total + term
        acc_ref[...] += total

    def inner_group(i, carry):
        base = 2 + i * GROUP
        js = [base + k for k in range(GROUP)]
        loads = [lambda part, span, j=j: x_ref[j, part, span] for j in js]
        group(js, [k % 2 for k in range(GROUP)], loads)
        return carry

    lax.fori_loop(0, (rows - 4) // GROUP, inner_group, 0)

    band_ref[...] = band()
    for k in range(8):
        rim_copy(0, k).wait()
        rim_copy(1, k).wait()

    def getter(wind, j):
        if j < 0:
            return row_of(north_ref, wind * 2 + j + 2)
        if j >= rows:
            return row_of(south_ref, wind * 2 + j - rows)
        k = j if j < 4 else j - rows + 8
        return lambda part: rim_ref[wind, k, part, :]

    edge_rows = (0, 1, rows - 2, rows - 1)
    for e, j in enumerate(edge_rows):

        def store(part, out, value, e=e):
            xe_ref[e, part, out * LANES : (out + 1) * LANES] = value

        near = [[getter(wind, j + d) for d in range(-2, 3)] for wind in range(2)]
        stencil_row(j, coef_ref, band_ref, *near, store, snaps, STENCIL_STEP)
    loads = [lambda part, span, e=e: xe_ref[e, part, span] for e in range(4)]
    group(list(edge_rows), [j % 2 for j in edge_rows], loads)

    low = acc_ref[:, snaps:]
    gram = acc_ref[:, :snaps] + (low + low.T)
    row = lax.broadcasted_iota(jnp.int32, (HALF, HALF), 0)
    col = lax.broadcasted_iota(jnp.int32, (HALF, HALF), 1)
    first = gram[:HALF, :HALF]
    second = gram[HALF:, HALF:]
    out_ref[0, :HALF, :] = gram[HALF:, :HALF]
    out_ref[1, :HALF, :] = jnp.where(row >= col, first, second)
    diagonal = jnp.sum(jnp.where(row == col, second, 0.0), axis=0, keepdims=True)
    out_ref[0, HALF:, :] = jnp.broadcast_to(diagonal, (8, HALF))
    out_ref[1, HALF:, :] = jnp.zeros((8, HALF), F32)


def partial_gram(x, west, east, from_west, from_east, north, south, u, v, scale, coef):
    rows, snaps, both = x.shape
    halves = VMEM((rows, snaps, both), BF16)
    return pl.pallas_call(
        functools.partial(gram_body, rows),
        out_shape=(halves, halves, VMEM((2, PIECE, HALF), F32)),
        in_specs=[vmem_spec()] * 7 + [any_spec()] * 2 + [vmem_spec(), smem_spec()],
        out_specs=(vmem_spec(),) * 3,
        scratch_shapes=[
            pltpu.VMEM((2, 2, snaps, LANES), F32),
            pltpu.VMEM((snaps, 2 * snaps), F32),
            pltpu.VMEM((2, 8, snaps, LANES), F32),
            pltpu.VMEM((4, snaps, both), F32),
            pltpu.VMEM((both, both), BF16),
            pltpu.SemaphoreType.DMA((2, 8)),
        ],
        compiler_params=pltpu.CompilerParams(vmem_limit_bytes=14 << 20),
        cost_estimate=cost(x.size * 1024, x.size * 8),
        name="partial_gram",
    )(
        *(in_vmem(y) for y in (x, west, east, from_west, from_east, north, south)),
        in_hbm(u), in_hbm(v), scale, coef,
    )


def swap(x, axis, bit):
    count = lax.axis_size(axis)
    return lax.ppermute(x, axis, [(i, i ^ bit) for i in range(count)])


def powers(count):
    bit = 1
    while bit < count:
        yield bit
        bit *= 2


def summed(parts):
    odd = lax.axis_index("lon") % 2 == 1
    mine = jnp.where(odd, parts[1], parts[0])
    other = jnp.where(odd, parts[0], parts[1])
    mine = mine + swap(other, "lon", 1)
    for bit in powers(lax.axis_size("lat")):
        mine = mine + swap(mine, "lat", bit)
    for bit in powers(lax.axis_size("lon")):
        if bit > 1:
            mine = mine + swap(mine, "lon", bit)
    theirs = swap(mine, "lon", 1)
    return jnp.where(odd, theirs, mine), jnp.where(odd, mine, theirs)


def dot_nt(a, b):
    return lax.dot_general(
        a, b, (((1,), (1,)), ((), ())), precision=lax.Precision.HIGHEST, preferred_element_type=F32
    )


def dot_nn(a, b):
    return lax.dot_general(
        a, b, (((1,), (0,)), ((), ())), precision=lax.Precision.HIGHEST, preferred_element_type=F32
    )


def eliminate(matrix, work_ref, right_ref):
    size = matrix.shape[0]
    groups = size // 8
    row = lax.broadcasted_iota(jnp.int32, (8, size), 0)
    col = lax.broadcasted_iota(jnp.int32, (8, size), 1)

    def spread(x, r):
        return jnp.broadcast_to(x[r : r + 1, :], x.shape)

    def columns(x, g):
        return [jnp.broadcast_to(x[:, 8 * g + r : 8 * g + r + 1], x.shape) for r in range(8)]

    work_ref[...] = matrix
    for g in range(groups):
        right_ref[8 * g : 8 * g + 8, :] = jnp.where(col == row + 8 * g, 1.0, 0.0)
    for g in range(groups):
        here = slice(8 * g, 8 * g + 8)
        work, right = work_ref[here, :], right_ref[here, :]
        cols = columns(work, g)
        steps = []
        for r in range(8):
            inverse = 1.0 / spread(cols[r], r)
            across = {c: spread(cols[c], r) for c in range(r + 1, 8)}
            work_row, right_row = spread(work, r), spread(right, r)
            steps.append((inverse, across, work_row, right_row))
            if r < 7:
                factor = jnp.where(row > r, cols[r] * inverse, 0.0)
                for c in range(r + 1, 8):
                    cols[c] = cols[c] - factor * across[c]
                work = work - factor * work_row
                right = right - factor * right_row
        work_ref[here, :] = work
        right_ref[here, :] = right
        for h in range(g + 1, groups):
            there = slice(8 * h, 8 * h + 8)
            work_h, right_h = work_ref[there, :], right_ref[there, :]
            cols_h = columns(work_h, g)
            for r in range(8):
                inverse, across, work_row, right_row = steps[r]
                factor = cols_h[r] * inverse
                for c in range(r + 1, 8):
                    cols_h[c] = cols_h[c] - factor * across[c]
                work_h = work_h - factor * work_row
                right_h = right_h - factor * right_row
            work_ref[there, :] = work_h
            right_ref[there, :] = right_h
    upper, lower = [], []
    for g in range(groups):
        here = slice(8 * g, 8 * g + 8)
        work, right = work_ref[here, :], right_ref[here, :]
        diagonal = jnp.sum(jnp.where(col == row + 8 * g, work, 0.0), axis=1, keepdims=True)
        root = lax.rsqrt(diagonal)
        upper.append(jnp.where(col >= row + 8 * g, work * root, 0.0))
        lower.append(right * root)
    return jnp.concatenate(upper, axis=0), jnp.concatenate(lower, axis=0)


def factor_body(total, corner_ref, mixed_ref, r_ref, hi_ref, lo_ref, work_ref, right_ref):
    inv = 1.0 / total
    row = lax.broadcasted_iota(jnp.int32, (HALF, HALF), 0)
    col = lax.broadcasted_iota(jnp.int32, (HALF, HALF), 1)
    mixed = mixed_ref[:HALF, :] * inv
    corner = corner_ref[:HALF, :] * inv
    diagonal = corner_ref[HALF : HALF + 1, :] * inv
    turned = mixed.T
    first = jnp.where(row >= col, mixed, turned)
    second = jnp.where(row < col, mixed, jnp.where(row > col, turned, diagonal))
    r11, w11 = eliminate(first, work_ref, right_ref)
    l21 = dot_nt(corner, w11)
    r22, w22 = eliminate(second - dot_nt(l21, l21), work_ref, right_ref)
    w21 = -dot_nn(w22, dot_nn(l21, w11))
    zero = jnp.zeros((HALF, HALF), F32)
    r_ref[:HALF, :HALF] = r11
    r_ref[:HALF, HALF:] = l21.T
    r_ref[HALF:, :HALF] = zero
    r_ref[HALF:, HALF:] = r22
    for i, j, w in ((0, 0, w11), (0, 1, zero), (1, 0, w21), (1, 1, w22)):
        part = (slice(i * HALF, (i + 1) * HALF), slice(j * HALF, (j + 1) * HALF))
        hi = w.astype(BF16)
        hi_ref[part] = hi
        lo_ref[part] = (w - hi.astype(F32)).astype(BF16)


def factor(corner, mixed, total):
    snaps = 2 * HALF
    return pl.pallas_call(
        functools.partial(factor_body, total),
        out_shape=(
            VMEM((snaps, snaps), F32),
            VMEM((snaps, snaps), BF16),
            VMEM((snaps, snaps), BF16),
        ),
        in_specs=[vmem_spec()] * 2,
        out_specs=(vmem_spec(),) * 3,
        scratch_shapes=[pltpu.VMEM((HALF, HALF), F32)] * 2,
        compiler_params=pltpu.CompilerParams(vmem_limit_bytes=12 << 20),
        cost_estimate=cost(1 << 26, 1 << 20),
        name="factor",
    )(in_vmem(corner), in_vmem(mixed))


def basis_body(rows, whi_ref, wlo_ref, hi_ref, lo_ref, r_ref, out_ref, r_out_ref, buf_ref, sems, r_sem):
    slots = buf_ref.shape[0]
    cols = out_ref.shape[3]

    def copy(j, slot, part):
        return pltpu.make_async_copy(
            buf_ref.at[slot, :, pl.ds(part * cols, cols)],
            out_ref.at[:, part, j, :],
            sems.at[slot, part],
        )

    pltpu.make_async_copy(r_ref, r_out_ref, r_sem).start()
    weights = jnp.concatenate([whi_ref[...], whi_ref[...], wlo_ref[...]], axis=1)

    def step(j, carry):
        slot = lax.rem(j, slots)

        @pl.when(j >= slots)
        def _():
            copy(j - slots, slot, 0).wait()
            copy(j - slots, slot, 1).wait()

        cells = jnp.concatenate([hi_ref[j], lo_ref[j], hi_ref[j]], axis=0)
        buf_ref[slot] = lax.dot_general(
            weights, cells, (((1,), (0,)), ((), ())), preferred_element_type=F32
        )
        copy(j, slot, 0).start()
        copy(j, slot, 1).start()
        return carry

    lax.fori_loop(0, rows, step, 0)

    def drain(j, carry):
        slot = lax.rem(j, slots)
        copy(j, slot, 0).wait()
        copy(j, slot, 1).wait()
        return carry

    lax.fori_loop(rows - slots, rows, drain, 0)
    pltpu.make_async_copy(r_ref, r_out_ref, r_sem).wait()


def basis(whi, wlo, hi, lo, r):
    rows, snaps, both = hi.shape
    cols = both // 2
    slots = 8
    return pl.pallas_call(
        functools.partial(basis_body, rows),
        out_shape=(
            jax.ShapeDtypeStruct((snaps, 2, rows, cols), F32),
            jax.ShapeDtypeStruct((snaps, snaps), F32),
        ),
        in_specs=[vmem_spec()] * 5,
        out_specs=(any_spec(), any_spec()),
        scratch_shapes=[
            pltpu.VMEM((slots, snaps, both), F32),
            pltpu.SemaphoreType.DMA((slots, 2)),
            pltpu.SemaphoreType.DMA(()),
        ],
        compiler_params=pltpu.CompilerParams(vmem_limit_bytes=8 << 20),
        cost_estimate=cost(hi.size * 1536, hi.size * 8),
        name="basis",
    )(in_vmem(whi), in_vmem(wlo), in_vmem(hi), in_vmem(lo), in_vmem(r))


def on_device(u, v):
    snaps, rows, cols = u.shape
    n_lat = rows * lax.axis_size("lat")
    lat, lon = lax.axis_size("lat"), lax.axis_size("lon")
    n_lon = cols * lon
    ratio = n_lon / (2.0 * n_lat)

    low, high = rims(u, v)
    north = lax.ppermute(high, "lat", [(i, i + 1) for i in range(lat - 1)])
    south = lax.ppermute(low, "lat", [(i + 1, i) for i in range(lat - 1)])
    u, v, _, _ = lax.optimization_barrier((u, v, low, high))

    index = (lax.axis_index("lat") * rows + jnp.arange(-2, rows + 2)).astype(F32)
    cosine = jnp.cos(-jnp.pi / 2 + (index + 0.5) * jnp.pi / n_lat)
    root = 1.0 / (12.0 * jnp.sqrt(cosine[2:-2]))
    along = ratio * root
    coef = jnp.stack(
        [
            along,
            8.0 * cosine[1:-3] * root,
            8.0 * cosine[3:-1] * root,
            cosine[:-4] * root,
            cosine[4:] * root,
        ],
        axis=1,
    )
    scale = jnp.broadcast_to(
        jnp.pad(jnp.repeat(along, 2), (0, LANES - 2 * rows))[None, :], (8, LANES)
    )

    west, east = edges(u, v)
    from_west = lax.ppermute(east, "lon", [(i, (i + 1) % lon) for i in range(lon)])
    from_east = lax.ppermute(west, "lon", [((i + 1) % lon, i) for i in range(lon)])
    x = differences(u, v, coef)
    hi, lo, parts = partial_gram(
        x, west, east, from_west, from_east, north, south, u, v, scale, coef
    )
    corner, mixed = summed(parts)
    r, whi, wlo = factor(corner, mixed, 2.0 * n_lat * n_lon)
    return basis(whi, wlo, hi, lo, r)


def solution(mesh):
    in_specs = (P(None, "lat", "lon"), P(None, "lat", "lon"))
    out_specs = (P(None, None, "lat", "lon"), P())
    return jax.shard_map(
        on_device, mesh=mesh, in_specs=in_specs, out_specs=out_specs, check_vma=False
    )
```

```python
import functools

import jax
import jax.numpy as jnp
import numpy as np
from jax import lax
from jax.experimental import pallas as pl
from jax.experimental.pallas import tpu as pltpu
from jax.sharding import PartitionSpec as P

F32 = jnp.float32
BF16 = jnp.bfloat16
VMEM = pltpu.MemorySpace.VMEM
LANES = 128
HALF = 128
PIECE = HALF + 8
GROUP = 4
GRAM_ROWS = 22


def vmem_spec():
    return pl.BlockSpec(memory_space=VMEM)


def smem_spec():
    return pl.BlockSpec(memory_space=pltpu.MemorySpace.SMEM)


def any_spec():
    return pl.BlockSpec(memory_space=pl.ANY)


def in_vmem(x):
    return pltpu.with_memory_space_constraint(x, VMEM)


def in_hbm(x):
    return pltpu.with_memory_space_constraint(x, pltpu.MemorySpace.HBM)


def cost(flops, nbytes):
    return pl.CostEstimate(flops=flops, bytes_accessed=nbytes, transcendentals=0)


def rim_body(rows, u_ref, v_ref, low_ref, high_ref, sems):
    def copy(k):
        wind, side, d = k // 4, k // 2 % 2, k % 2
        row = d if side == 0 else rows - 2 + d
        return pltpu.make_async_copy(
            (u_ref, v_ref)[wind].at[:, row, :],
            (low_ref, high_ref)[side].at[2 * wind + d],
            sems.at[k],
        )

    for k in range(8):
        copy(k).start()
    for k in range(8):
        copy(k).wait()


def rims(u, v):
    snaps, rows, cols = u.shape
    rim = VMEM((4, snaps, cols), F32)
    return pl.pallas_call(
        functools.partial(rim_body, rows),
        out_shape=(rim, rim),
        in_specs=[any_spec(), any_spec()],
        out_specs=(vmem_spec(),) * 2,
        scratch_shapes=[pltpu.SemaphoreType.DMA((8,))],
        compiler_params=pltpu.CompilerParams(vmem_limit_bytes=1 << 20),
        cost_estimate=cost(0, 1 << 22),
        name="rims",
    )(in_hbm(u), in_hbm(v))


def row_copy(u_ref, v_ref, ut_ref, vt_ref, sems):
    def copy(wind, j):
        src = (u_ref, v_ref)[wind]
        dst = (ut_ref, vt_ref)[wind]
        return pltpu.make_async_copy(src.at[:, j, :], dst.at[j], sems.at[wind, j])

    def start(j, carry):
        copy(0, j).start()
        copy(1, j).start()
        return carry

    return copy, start


TABLE = 1024
TAPS = 5


def table_copy(table_ref, coef_ref, sem):
    here = pl.multiple_of(lax.axis_index("lat") * TABLE, TABLE)
    return pltpu.make_async_copy(table_ref.at[pl.ds(here, TABLE)], coef_ref, sem)


def band():
    size = 2 * LANES
    k = lax.broadcasted_iota(jnp.int32, (size, size), 0)
    n = lax.broadcasted_iota(jnp.int32, (size, size), 1)
    inside = jnp.logical_and((k >> 7) == (n >> 7), (k & (LANES - 1)) < LANES - 2)
    d = n - k
    taps = jnp.where(d == 1, 8.0, jnp.where(jnp.logical_or(d == 0, d == 2), -1.0, 0.0))
    return jnp.where(inside, taps, 0.0).astype(BF16)


def split(x):
    hi = x.astype(BF16)
    return hi, (x - hi.astype(F32)).astype(BF16)


def stencil_row(j, coef_ref, band_ref, u_near, v_near, store, snaps, step):
    lon, *lat = [coef_ref[TAPS * j + k] for k in range(TAPS)]

    def across(near, part):
        return (lat[1] * near[3](part) - lat[0] * near[1](part)) - (
            lat[3] * near[4](part) - lat[2] * near[0](part)
        )

    for t in range(0, snaps, step):
        part = pl.ds(t, step)
        ahead = []
        for near in (v_near, u_near):
            cells = near[2](part)
            ahead.append(pltpu.roll(cells, LANES - 2, 1) - cells)
        hi, lo = split(jnp.concatenate(ahead, axis=1))
        both = lax.dot_general(
            jnp.concatenate([lo, hi], axis=0),
            band_ref[...],
            (((1,), (0,)), ((), ())),
            preferred_element_type=F32,
        )
        along = both[:step] + both[step:]
        store(part, 0, lon * along[:, :LANES] - across(u_near, part))
        store(part, 1, lon * along[:, LANES:] + across(v_near, part))


def row_of(ref, j):
    return lambda part: ref[j, part, :]


def store_row(x_ref, j):
    def store(part, out, value):
        x_ref[j, part, out * LANES : (out + 1) * LANES] = value

    return store


def near_rows(ut_ref, vt_ref, j):
    return [[row_of(ref, j + d) for d in range(-2, 3)] for ref in (ut_ref, vt_ref)]


STENCIL_STEP = 128


def edge_body(
    rows, u_ref, v_ref, lanes_ref, west_ref, east_ref, scale_ref, ut_ref, vt_ref, sems, extra
):
    snaps = u_ref.shape[0]
    copy, start = row_copy(u_ref, v_ref, ut_ref, vt_ref, sems)
    lax.fori_loop(0, GROUP, start, 0)
    get_scale = pltpu.make_async_copy(lanes_ref.at[lax.axis_index("lat")], scale_ref, extra)
    get_scale.start()
    lax.fori_loop(GROUP, rows, start, 0)
    step = 32
    lane = lax.broadcasted_iota(jnp.int32, (step, LANES), 1)
    for wind in range(2):
        west_ref[wind] = jnp.zeros((snaps, LANES), F32)
        east_ref[wind] = jnp.zeros((snaps, LANES), F32)

    def pack(base):
        for wind in range(2):
            src = (ut_ref, vt_ref)[wind]
            for t in range(0, snaps, step):
                part = pl.ds(t, step)
                west, east = west_ref[wind, part, :], east_ref[wind, part, :]
                for k in range(GROUP):
                    j = base + k
                    turned = pltpu.roll(src[j, part, :], 2 * j + 2, 1)
                    west = jnp.where((lane >> 1) == j + 1, turned, west)
                    east = jnp.where((lane >> 1) == j, turned, east)
                west_ref[wind, part, :] = west
                east_ref[wind, part, :] = east

    def arrived(base):
        for k in range(GROUP):
            copy(0, base + k).wait()
            copy(1, base + k).wait()

    def body(i, carry):
        arrived(i * GROUP)
        pack(i * GROUP)
        return carry

    lax.fori_loop(0, rows // GROUP, body, 0)
    get_scale.wait()


def edges(u, v, lanes):
    snaps, rows, cols = u.shape
    packed = VMEM((2, snaps, LANES), F32)
    return pl.pallas_call(
        functools.partial(edge_body, rows),
        out_shape=(packed, packed, VMEM((8, LANES), F32)),
        in_specs=[any_spec()] * 3,
        out_specs=(vmem_spec(),) * 3,
        scratch_shapes=[
            pltpu.VMEM((rows, snaps, cols), F32),
            pltpu.VMEM((rows, snaps, cols), F32),
            pltpu.SemaphoreType.DMA((2, rows)),
            pltpu.SemaphoreType.DMA(()),
        ],
        compiler_params=pltpu.CompilerParams(vmem_limit_bytes=16 << 20),
        cost_estimate=cost(u.size * 8, u.size * 8),
        name="edges",
    )(in_hbm(u), in_hbm(v), in_hbm(lanes))


STENCIL_ROWS = 4


def stencil_body(
    rows, u_ref, v_ref, table_ref, x_ref,
    ut_ref, vt_ref, band_ref, coef_ref, sems, extra,
):
    snaps = u_ref.shape[0]
    first = 2
    copy, start = row_copy(u_ref, v_ref, ut_ref, vt_ref, sems)
    get_coef = table_copy(table_ref, coef_ref, extra)
    lax.fori_loop(first - 2, first + 2, start, 0)
    get_coef.start()
    lax.fori_loop(first + 2, rows, start, 0)
    band_ref[...] = band()

    def arrived(j):
        copy(0, j).wait()
        copy(1, j).wait()

    def middle(i, carry):
        base = first + i * STENCIL_ROWS
        for r in range(STENCIL_ROWS):
            arrived(base + r + 2)
        for r in range(STENCIL_ROWS):
            j = base + r
            near = near_rows(ut_ref, vt_ref, j)
            stencil_row(
                j, coef_ref, band_ref, *near, store_row(x_ref, j - first), snaps, STENCIL_STEP
            )
        return carry

    for j in range(first - 2, first + 2):
        arrived(j)
    get_coef.wait()
    lax.fori_loop(0, (rows - 4) // STENCIL_ROWS, middle, 0)


def differences(u, v, table):
    snaps, rows, cols = u.shape
    return pl.pallas_call(
        functools.partial(stencil_body, rows),
        out_shape=VMEM((rows - 4, snaps, 2 * cols), F32),
        in_specs=[any_spec()] * 3,
        out_specs=vmem_spec(),
        scratch_shapes=[
            pltpu.VMEM((rows, snaps, cols), F32),
            pltpu.VMEM((rows, snaps, cols), F32),
            pltpu.VMEM((2 * LANES, 2 * LANES), BF16),
            pltpu.SMEM((TABLE,), F32),
            pltpu.SemaphoreType.DMA((2, rows)),
            pltpu.SemaphoreType.DMA(()),
        ],
        compiler_params=pltpu.CompilerParams(vmem_limit_bytes=18 << 20),
        cost_estimate=cost(u.size * 2048, u.size * 16),
        name="differences",
    )(in_hbm(u), in_hbm(v), in_hbm(table))


def gram_body(
    rows, x_ref, west_ref, east_ref, from_west_ref, from_east_ref, north_ref, south_ref,
    scale_ref, u_ref, v_ref, table_ref,
    hi_ref, lo_ref, out_ref,
    fix_ref, acc_ref, rim_ref, xe_ref, band_ref, coef_ref, sems, extra,
):
    snaps = x_ref.shape[1]
    step = 64

    def rim_copy(wind, k):
        row = k if k < 4 else rows - 8 + k
        return pltpu.make_async_copy(
            (u_ref, v_ref)[wind].at[:, row, :], rim_ref.at[wind, k], sems.at[wind, k]
        )

    get_coef = table_copy(table_ref, coef_ref, extra)
    get_coef.start()
    for k in range(8):
        rim_copy(0, k).start()
        rim_copy(1, k).start()
    lane = lax.broadcasted_iota(jnp.int32, (step, LANES), 1)
    even = lane % 2 == 0
    even_row = (lane // 2) % 2 == 0
    scale = scale_ref[0:1, :]
    for wind in range(2):
        for t in range(0, snaps, step):
            part = pl.ds(t, step)
            left = pltpu.roll(west_ref[wind, part, :], LANES - 2, 1) - from_west_ref[wind, part, :]
            right = pltpu.roll(from_east_ref[wind, part, :], LANES - 2, 1) - east_ref[wind, part, :]
            left = scale * (jnp.where(even, 8.0 * pltpu.roll(left, LANES - 1, 1), 0.0) - left)
            right = scale * (jnp.where(even, 0.0, 8.0 * pltpu.roll(right, 1, 1)) - right)
            right = pltpu.roll(right, LANES - 2, 1)
            fix_ref[wind, 0, part, :] = jnp.where(even_row, left, right)
            fix_ref[wind, 1, part, :] = jnp.where(even_row, right, left)
    acc_ref[...] = jnp.zeros_like(acc_ref)
    outer = jnp.logical_or(lane < 2, lane >= LANES - 2)

    def group(row_list, parities, loads):
        for j, parity, load in zip(row_list, parities, loads):
            shift = (2 * LANES - 2 * j) % LANES
            for out in range(2):
                for t in range(0, snaps, step):
                    part = pl.ds(t, step)
                    fix = pltpu.roll(fix_ref[1 - out, parity, part, :], shift, 1)
                    span = slice(out * LANES, (out + 1) * LANES)
                    x = load(part, span) + jnp.where(outer, fix, 0.0)
                    hi, lo = split(x)
                    hi_ref[j, part, span] = hi
                    lo_ref[j, part, span] = lo
        total = None
        for j in row_list:
            hi = hi_ref[j]
            both = jnp.concatenate([hi, lo_ref[j]], axis=0)
            term = lax.dot_general(
                hi, both, (((1,), (1,)), ((), ())), preferred_element_type=F32
            )
            total = term if total is None else total + term
        acc_ref[...] += total

    def inner_group(i, carry):
        base = i * GRAM_ROWS
        loads = [
            lambda part, span, k=base + k: x_ref[k, part, span] for k in range(GRAM_ROWS)
        ]
        js = [base + k + 2 for k in range(GRAM_ROWS)]
        group(js, [k % 2 for k in range(GRAM_ROWS)], loads)
        return carry

    lax.fori_loop(0, (rows - 4) // GRAM_ROWS, inner_group, 0)

    band_ref[...] = band()
    get_coef.wait()
    for k in range(8):
        rim_copy(0, k).wait()
        rim_copy(1, k).wait()

    def getter(wind, j):
        if j < 0:
            return row_of(north_ref, wind * 2 + j + 2)
        if j >= rows:
            return row_of(south_ref, wind * 2 + j - rows)
        k = j if j < 4 else j - rows + 8
        return lambda part: rim_ref[wind, k, part, :]

    edge_rows = (0, 1, rows - 2, rows - 1)
    for e, j in enumerate(edge_rows):
        near = [[getter(wind, j + d) for d in range(-2, 3)] for wind in range(2)]
        stencil_row(j, coef_ref, band_ref, *near, store_row(xe_ref, e), snaps, STENCIL_STEP)
    loads = [lambda part, span, e=e: xe_ref[e, part, span] for e in range(4)]
    group(list(edge_rows), [j % 2 for j in edge_rows], loads)

    low = acc_ref[:, snaps:]
    gram = acc_ref[:, :snaps] + (low + low.T)
    row = lax.broadcasted_iota(jnp.int32, (HALF, HALF), 0)
    col = lax.broadcasted_iota(jnp.int32, (HALF, HALF), 1)
    first = gram[:HALF, :HALF]
    second = gram[HALF:, HALF:]
    out_ref[0, :HALF, :] = gram[HALF:, :HALF]
    out_ref[1, :HALF, :] = jnp.where(row >= col, first, second)
    diagonal = jnp.sum(jnp.where(row == col, second, 0.0), axis=0, keepdims=True)
    out_ref[0, HALF:, :] = jnp.broadcast_to(diagonal, (8, HALF))
    out_ref[1, HALF:, :] = jnp.zeros((8, HALF), F32)


def partial_gram(x, west, east, from_west, from_east, north, south, scale, u, v, table):
    snaps, rows, cols = u.shape
    both = 2 * cols
    halves = VMEM((rows, snaps, both), BF16)
    return pl.pallas_call(
        functools.partial(gram_body, rows),
        out_shape=(halves, halves, VMEM((2, PIECE, HALF), F32)),
        in_specs=[vmem_spec()] * 8 + [any_spec()] * 3,
        out_specs=(vmem_spec(),) * 3,
        scratch_shapes=[
            pltpu.VMEM((2, 2, snaps, LANES), F32),
            pltpu.VMEM((snaps, 2 * snaps), F32),
            pltpu.VMEM((2, 8, snaps, LANES), F32),
            pltpu.VMEM((4, snaps, both), F32),
            pltpu.VMEM((both, both), BF16),
            pltpu.SMEM((TABLE,), F32),
            pltpu.SemaphoreType.DMA((2, 8)),
            pltpu.SemaphoreType.DMA(()),
        ],
        compiler_params=pltpu.CompilerParams(vmem_limit_bytes=14 << 20),
        cost_estimate=cost(u.size * 2048, u.size * 16),
        name="partial_gram",
    )(
        *(
            in_vmem(y)
            for y in (x, west, east, from_west, from_east, north, south, scale)
        ),
        in_hbm(u), in_hbm(v), in_hbm(table),
    )


def swap(x, axis, bit):
    count = lax.axis_size(axis)
    return lax.ppermute(x, axis, [(i, i ^ bit) for i in range(count)])


def bits_from(first, count):
    bits = []
    while first < count:
        bits.append(first)
        first *= 2
    return bits


def summed_over(x, axis, bits):
    while bits:
        if len(bits) > 1:
            one, two, bits = bits[0], bits[1], bits[2:]
            near, far, both = (swap(x, axis, b) for b in (one, two, one + two))
            x = (x + near) + (far + both)
        else:
            x, bits = x + swap(x, axis, bits[0]), []
    return x


def summed(parts):
    odd = lax.axis_index("lon") % 2 == 1
    mine = jnp.where(odd, parts[1], parts[0])
    other = jnp.where(odd, parts[0], parts[1])
    mine = mine + swap(other, "lon", 1)
    mine = summed_over(mine, "lon", bits_from(2, lax.axis_size("lon")))
    mine = summed_over(mine, "lat", bits_from(1, lax.axis_size("lat")))
    theirs = swap(mine, "lon", 1)
    return jnp.where(odd, theirs, mine), jnp.where(odd, mine, theirs)


def dot_nt(a, b):
    return lax.dot_general(
        a, b, (((1,), (1,)), ((), ())), precision=lax.Precision.HIGHEST, preferred_element_type=F32
    )


def dot_nn(a, b):
    return lax.dot_general(
        a, b, (((1,), (0,)), ((), ())), precision=lax.Precision.HIGHEST, preferred_element_type=F32
    )


def eliminate(matrix, work_ref, right_ref):
    size = matrix.shape[0]
    groups = size // 8
    row = lax.broadcasted_iota(jnp.int32, (8, size), 0)
    col = lax.broadcasted_iota(jnp.int32, (8, size), 1)

    def spread(x, r):
        return jnp.broadcast_to(x[r : r + 1, :], x.shape)

    def columns(x, g):
        return [jnp.broadcast_to(x[:, 8 * g + r : 8 * g + r + 1], x.shape) for r in range(8)]

    work_ref[...] = matrix
    for g in range(groups):
        right_ref[8 * g : 8 * g + 8, :] = jnp.where(col == row + 8 * g, 1.0, 0.0)
    for g in range(groups):
        here = slice(8 * g, 8 * g + 8)
        work, right = work_ref[here, :], right_ref[here, :]
        cols = columns(work, g)
        steps = []
        for r in range(8):
            inverse = spread(1.0 / cols[r], r)
            across = {c: spread(cols[c], r) for c in range(r + 1, 8)}
            work_row, right_row = spread(work, r), spread(right, r)
            steps.append((inverse, across, work_row, right_row))
            if r < 7:
                factor = jnp.where(row > r, cols[r] * inverse, 0.0)
                for c in range(r + 1, 8):
                    cols[c] = cols[c] - factor * across[c]
                work = work - factor * work_row
                right = right - factor * right_row
        work_ref[here, :] = work
        right_ref[here, :] = right
        for h in range(g + 1, groups):
            there = slice(8 * h, 8 * h + 8)
            work_h, right_h = work_ref[there, :], right_ref[there, :]
            cols_h = columns(work_h, g)
            for r in range(8):
                inverse, across, work_row, right_row = steps[r]
                factor = cols_h[r] * inverse
                for c in range(r + 1, 8):
                    cols_h[c] = cols_h[c] - factor * across[c]
                work_h = work_h - factor * work_row
                right_h = right_h - factor * right_row
            work_ref[there, :] = work_h
            right_ref[there, :] = right_h
    upper, lower = [], []
    for g in range(groups):
        here = slice(8 * g, 8 * g + 8)
        work, right = work_ref[here, :], right_ref[here, :]
        diagonal = jnp.sum(jnp.where(col == row + 8 * g, work, 0.0), axis=1, keepdims=True)
        root = lax.rsqrt(diagonal)
        upper.append(jnp.where(col >= row + 8 * g, work * root, 0.0))
        lower.append(right * root)
    return jnp.concatenate(upper, axis=0), jnp.concatenate(lower, axis=0)


def factor_body(total, corner_ref, mixed_ref, r_ref, hi_ref, lo_ref, work_ref, right_ref):
    inv = 1.0 / total
    row = lax.broadcasted_iota(jnp.int32, (HALF, HALF), 0)
    col = lax.broadcasted_iota(jnp.int32, (HALF, HALF), 1)
    mixed = mixed_ref[:HALF, :] * inv
    corner = corner_ref[:HALF, :] * inv
    diagonal = corner_ref[HALF : HALF + 1, :] * inv
    turned = mixed.T
    first = jnp.where(row >= col, mixed, turned)
    second = jnp.where(row < col, mixed, jnp.where(row > col, turned, diagonal))
    r11, w11 = eliminate(first, work_ref, right_ref)
    l21 = dot_nt(corner, w11)
    r22, w22 = eliminate(second - dot_nt(l21, l21), work_ref, right_ref)
    w21 = -dot_nn(w22, dot_nn(l21, w11))
    zero = jnp.zeros((HALF, HALF), F32)
    r_ref[:HALF, :HALF] = r11
    r_ref[:HALF, HALF:] = l21.T
    r_ref[HALF:, :HALF] = zero
    r_ref[HALF:, HALF:] = r22
    for i, j, w in ((0, 0, w11), (0, 1, zero), (1, 0, w21), (1, 1, w22)):
        part = (slice(i * HALF, (i + 1) * HALF), slice(j * HALF, (j + 1) * HALF))
        hi = w.astype(BF16)
        hi_ref[part] = hi
        lo_ref[part] = (w - hi.astype(F32)).astype(BF16)


def factor(corner, mixed, total):
    snaps = 2 * HALF
    return pl.pallas_call(
        functools.partial(factor_body, total),
        out_shape=(
            VMEM((snaps, snaps), F32),
            VMEM((snaps, snaps), BF16),
            VMEM((snaps, snaps), BF16),
        ),
        in_specs=[vmem_spec()] * 2,
        out_specs=(vmem_spec(),) * 3,
        scratch_shapes=[pltpu.VMEM((HALF, HALF), F32)] * 2,
        compiler_params=pltpu.CompilerParams(vmem_limit_bytes=12 << 20),
        cost_estimate=cost(1 << 26, 1 << 20),
        name="factor",
    )(in_vmem(corner), in_vmem(mixed))


def basis_body(rows, whi_ref, wlo_ref, hi_ref, lo_ref, r_ref, out_ref, r_out_ref, buf_ref, sems, r_sem):
    slots = buf_ref.shape[0]
    cols = out_ref.shape[3]

    def copy(j, slot, part):
        return pltpu.make_async_copy(
            buf_ref.at[slot, :, pl.ds(part * cols, cols)],
            out_ref.at[:, part, j, :],
            sems.at[slot, part],
        )

    pltpu.make_async_copy(r_ref, r_out_ref, r_sem).start()
    full, top = jnp.concatenate([whi_ref[...], wlo_ref[...]], axis=0), whi_ref[...]
    snaps = top.shape[0]

    def dot(a, b):
        return lax.dot_general(a, b, (((1,), (0,)), ((), ())), preferred_element_type=F32)

    def step(i, carry):
        js = [i * BASIS_ROWS + k for k in range(BASIS_ROWS)]
        for j in js:

            @pl.when(j >= slots)
            def _(j=j):
                for part in range(2):
                    copy(j - slots, lax.rem(j, slots), part).wait()

        for j in js:
            main = dot(full, hi_ref[j])
            buf_ref[lax.rem(j, slots)] = main[:snaps] + (main[snaps:] + dot(top, lo_ref[j]))
        for j in js:
            for part in range(2):
                copy(j, lax.rem(j, slots), part).start()
        return carry

    lax.fori_loop(0, rows // BASIS_ROWS, step, 0)

    def drain(j, carry):
        slot = lax.rem(j, slots)
        copy(j, slot, 0).wait()
        copy(j, slot, 1).wait()
        return carry

    lax.fori_loop(rows - slots, rows, drain, 0)
    pltpu.make_async_copy(r_ref, r_out_ref, r_sem).wait()


BASIS_ROWS = 8


def basis(whi, wlo, hi, lo, r):
    rows, snaps, both = hi.shape
    cols = both // 2
    slots = 2 * BASIS_ROWS
    return pl.pallas_call(
        functools.partial(basis_body, rows),
        out_shape=(
            jax.ShapeDtypeStruct((snaps, 2, rows, cols), F32),
            jax.ShapeDtypeStruct((snaps, snaps), F32),
        ),
        in_specs=[vmem_spec()] * 5,
        out_specs=(any_spec(), any_spec()),
        scratch_shapes=[
            pltpu.VMEM((slots, snaps, both), F32),
            pltpu.SemaphoreType.DMA((slots, 2)),
            pltpu.SemaphoreType.DMA(()),
        ],
        compiler_params=pltpu.CompilerParams(vmem_limit_bytes=8 << 20),
        cost_estimate=cost(hi.size * 1536, hi.size * 8),
        name="basis",
    )(in_vmem(whi), in_vmem(wlo), in_vmem(hi), in_vmem(lo), in_vmem(r))


def on_device(u, v):
    snaps, rows, cols = u.shape
    n_lat = rows * lax.axis_size("lat")
    lat, lon = lax.axis_size("lat"), lax.axis_size("lon")
    n_lon = cols * lon
    ratio = n_lon / (2.0 * n_lat)

    low, high = rims(u, v)
    north = lax.ppermute(high, "lat", [(i, i + 1) for i in range(lat - 1)])
    south = lax.ppermute(low, "lat", [(i + 1, i) for i in range(lat - 1)])
    u, v, _, _ = lax.optimization_barrier((u, v, low, high))

    index = np.arange(-2, n_lat + 2, dtype=np.float64)
    cosine = np.cos(-np.pi / 2 + (index + 0.5) * np.pi / n_lat)
    root = 1.0 / (12.0 * np.sqrt(cosine[2:-2]))
    along = ratio * root
    table = np.stack(
        [
            along,
            8.0 * cosine[1:-3] * root,
            8.0 * cosine[3:-1] * root,
            cosine[:-4] * root,
            cosine[4:] * root,
        ],
        axis=1,
    ).reshape(lat, rows * TAPS)
    table = jnp.asarray(np.pad(table, ((0, 0), (0, TABLE - rows * TAPS))).reshape(-1), F32)
    lanes = np.zeros((lat, 8, LANES))
    lanes[:, :, : 2 * rows] = np.repeat(along.reshape(lat, rows), 2, axis=1)[:, None, :]
    lanes = jnp.asarray(lanes, F32)

    west, east, scale = edges(u, v, lanes)
    from_west = lax.ppermute(east, "lon", [(i, (i + 1) % lon) for i in range(lon)])
    from_east = lax.ppermute(west, "lon", [((i + 1) % lon, i) for i in range(lon)])
    x = differences(u, v, table)
    hi, lo, parts = partial_gram(
        x, west, east, from_west, from_east, north, south, scale, u, v, table
    )
    corner, mixed = summed(parts)
    r, whi, wlo = factor(corner, mixed, 2.0 * n_lat * n_lon)
    return basis(whi, wlo, hi, lo, r)


def solution(mesh):
    in_specs = (P(None, "lat", "lon"), P(None, "lat", "lon"))
    out_specs = (P(None, None, "lat", "lon"), P())
    return jax.shard_map(
        on_device, mesh=mesh, in_specs=in_specs, out_specs=out_specs, check_vma=False
    )
```
